128 devices in a mesh: theta: 16 (over z_hi, y, core), rad: 8 (over x, z_lo).
Axes of the slice: x: 4, y: 4, z: 4 (z_hi: 2, z_lo: 2; z = z_hi * 2 + z_lo), core: 2. Of those that a mesh axis runs over, the one named last changes fastest.
Arguments:
- velocity: float32 [3, 8, 8192, 1024], P(None, None, 'theta', 'rad'), may hold values from -6 to 6
- radial_inverse: float32 [3, 1024, 1024], replicated, may hold values from -1 to 1.5, as said below
Outputs:
- advanced: float32 [3, 8, 8192, 1024], P(None, None, 'theta', 'rad')
The draws below stay inside these ranges and needn't reach their ends.
Inputs may be any that keep to these rules, and one draw needn't show every extreme that they name: `radial_inverse`: diagonal entries lie in 1 to 1.5, off-diagonal ones in -0.8 to 0.8.
All inputs are finite; a program needn't handle non-finite values.
Results may differ from the reference program's by a relative error of at most 0.000071.
Values sent between devices are 32-bit elements; how exact they have to be, the bound alone decides.
No kernel may reach another device: no remote copies, remote signals or barrier semaphores. Data moves between devices by JAX's collectives and lax.ppermute only.
A program may use at most 128 MiB of HBM per device.

```python
import math
import jax
import jax.numpy as jnp
from jax import lax

NR = 1024
PLANES = 8
NT = 8192


def draw_radial_inverse(key, part):
    key_noise, key_diag = jax.random.split(key, 2)
    index = jnp.arange(NR)
    distance = jnp.abs(index[:, None] - index[None, :]).astype(jnp.float32)
    base = jnp.exp(-distance / (NR / 4.0))
    noise = jax.random.truncated_normal(key_noise, -3.0, 3.0, (3, NR, NR), jnp.float32)
    identity = jnp.eye(NR, dtype=jnp.float32)
    offdiag = 2.0 / math.sqrt(NR) * base * noise * (1.0 - identity)
    diagonal = identity * (1.0 + 0.5 * jax.random.uniform(key_diag, (3, NR, NR), jnp.float32))
    value = offdiag + diagonal
    return value


def block_scale(stream_key, dims, cuts, smallest, largest):
    factor_of = 1.0
    for position, shards_of in cuts:
        draws = jax.random.uniform(jax.random.fold_in(jax.random.fold_in(stream_key, 6), position), (shards_of,), jnp.float32, smallest / len(cuts), largest / len(cuts))
        factor_of = factor_of * jnp.repeat(jnp.exp(draws), dims[position] // shards_of).reshape((-1,) + (1,) * (len(dims) - 1 - position))
    return factor_of


def scatter_about(rng, extent, spread, bound, cuts=(), kind=jnp.bfloat16):
    drawn = jax.random.normal(rng, extent, jnp.float32) * spread
    if len(cuts) > 0:
        drawn = block_scale(rng, extent, cuts, -0.22, 0.18) * drawn
    return jnp.clip(drawn, min=-bound, max=bound).astype(kind)


def setup_inputs(seed: int = 0) -> dict:
    key_list = jax.random.split(jax.random.key(seed), 3)
    return {
        "velocity": scatter_about(key_list[0], (3, PLANES, NT, NR), 1.0, 6.0, ((2, 16), (3, 8)), jnp.float32),
        "radial_inverse": draw_radial_inverse(jax.random.fold_in(key_list[2], 71), 0),
    }


courant = 0.25
viscous = 0.05


def plane_step(plane, radial_inverse, radius):
    plus_one = jnp.roll(plane, -1, axis=1)
    plus_two = jnp.roll(plane, -2, axis=1)
    minus_one = jnp.roll(plane, 1, axis=1)
    minus_two = jnp.roll(plane, 2, axis=1)
    first = (-plus_two + 8.0 * plus_one - 8.0 * minus_one + minus_two) / 12.0
    second = (-plus_two + 16.0 * plus_one - 30.0 * plane + 16.0 * minus_one - minus_two) / 12.0
    swirl = plane[1]
    rhs = plane - courant * (swirl / radius)[None] * first + viscous * second / (radius * radius)
    weighted = rhs * radius
    solved = jnp.einsum("ctk,cik->cti", weighted, radial_inverse, precision=lax.Precision.HIGHEST)
    return solved / radius


def reference(velocity, radial_inverse):
    radius = 1.0 + (jnp.arange(NR).astype(jnp.float32) + 0.5) / NR
    planes = jnp.moveaxis(velocity, 1, 0)
    result = lax.map(lambda plane: plane_step(plane, radial_inverse, radius), planes)
    return jnp.moveaxis(result, 0, 1)
```

```python
import functools
import jax
import jax.numpy as jnp
from jax import lax
from jax.experimental import pallas as pl
from jax.experimental.pallas import tpu as pltpu
from jax.sharding import PartitionSpec as P

NR = 1024
courant = 0.25
viscous = 0.05
LENGTH = 512
HOPS = ((0, 0), (1, 0), (3, 0), (0, 1), (2, 0), (1, 1), (3, 1), (2, 1))
CHUNKS = ((128, 32, False), (0, 32, True))
MIB = 1 << 20


def whole():
    return pl.BlockSpec(memory_space=pltpu.VMEM)


def anywhere():
    return pl.BlockSpec(memory_space=pl.ANY)


def piece(per):
    return jax.ShapeDtypeStruct((3, 8, per, 128), jnp.float32)


def peers(sign):
    me = lax.axis_index("rad")
    x, z = me // 2, me % 2
    return [lax.rem(x + (4 + sign * dx) % 4, 4) * 2 + (z + dz) % 2 for dx, dz in HOPS]


def pairs(dx, dz):
    return [(x * 2 + z, (x + dx) % 4 * 2 + (z + dz) % 2) for x in range(4) for z in range(2)]


def row_of(chunk, owner):
    first, per, ends = chunk
    if ends:
        return owner * per + jnp.where(owner >= 4, LENGTH - 8 * per, 0)
    return first + owner * per


def stencil_kernel(chunk, *refs):
    first, per, ends = chunk
    if ends:
        velocity, below, above, coef, *outs, ext, sems = refs
    else:
        velocity, coef, *outs, ext, sems = refs
    half = 4 * per

    def copies(z):
        at = [velocity.at[:, z]]
        if ends:
            return [
                pltpu.make_async_copy(below.at[:, z], ext.at[:, z, pl.ds(0, 8)], sems.at[z, 0]),
                pltpu.make_async_copy(at[0].at[:, pl.ds(0, half + 8)], ext.at[:, z, pl.ds(8, half + 8)], sems.at[z, 1]),
                pltpu.make_async_copy(at[0].at[:, pl.ds(LENGTH - half - 8, half + 8)], ext.at[:, z, pl.ds(half + 16, half + 8)], sems.at[z, 2]),
                pltpu.make_async_copy(above.at[:, z], ext.at[:, z, pl.ds(2 * half + 24, 8)], sems.at[z, 3]),
            ]
        return [pltpu.make_async_copy(at[0].at[:, pl.ds(first - 8, 8 * per + 16)], ext.at[:, z], sems.at[z, 0])]

    for z in range(8):
        for copy in copies(z):
            copy.start()
    to = peers(1)

    @pl.loop(0, 8)
    def _(z):
        for copy in copies(z):
            copy.wait()
        c_mid = coef[0:1, :]
        c_out = coef[1:2, :]
        for d in range(8):
            owner = to[d]
            start = owner * per
            if ends:
                start = start + jnp.where(owner >= 4, 16, 0)
            start = pl.multiple_of(start, 8)
            around = [ext[c, z, pl.ds(start, per + 16), :] for c in range(3)]
            swirl = around[1][8 : 8 + per] * (courant / 12.0)
            for c in range(3):
                m2, m1, mid, p1, p2 = (around[c][8 + k : 8 + k + per] for k in range(-2, 3))
                along = 8.0 * (p1 - m1) - (p2 - m2)
                outer = 16.0 * (p1 + m1) - (p2 + m2)
                outs[d][c, z] = mid * c_mid - swirl * along + outer * c_out


def stencil(chunk, velocity, below, above, coef):
    first, per, ends = chunk
    halos = (below, above) if ends else ()
    return pl.pallas_call(
        functools.partial(stencil_kernel, chunk),
        in_specs=[anywhere()] * (1 + len(halos)) + [whole()],
        out_specs=[whole()] * 8,
        out_shape=[piece(per)] * 8,
        scratch_shapes=[
            pltpu.VMEM((3, 8, 8 * per + (32 if ends else 16), 128), jnp.float32),
            pltpu.SemaphoreType.DMA((8, 4)),
        ],
        cost_estimate=pl.CostEstimate(flops=3 * 8 * 8 * per * 128 * 13, bytes_accessed=2 * 3 * 8 * 8 * per * 128 * 4, transcendentals=0),
        compiler_params=pltpu.CompilerParams(vmem_limit_bytes=16 * MIB),
        name="stencil",
    )(velocity, *halos, coef)


def prepare_kernel(m_ref, hi_ref, lo_ref):
    rows = m_ref.shape[1]
    at = pl.program_id(1) * rows
    index = at + lax.broadcasted_iota(jnp.int32, (rows, 128), 0)
    scale = 1.0 / (1.0 + (index.astype(jnp.float32) + 0.5) / NR)
    for k in range(NR // 128):
        block = m_ref[0, :, k * 128 : (k + 1) * 128] * scale
        turned = block.T
        hi = turned.astype(jnp.bfloat16)
        hi_ref[0, k * 128 : (k + 1) * 128, :] = hi
        lo_ref[0, k * 128 : (k + 1) * 128, :] = (turned - hi.astype(jnp.float32)).astype(jnp.bfloat16)


def prepare(radial_inverse):
    rows = 256
    spec = pl.BlockSpec((1, NR, rows), lambda c, i: (c, 0, i))
    shape = jax.ShapeDtypeStruct((3, NR, NR), jnp.bfloat16)
    return pl.pallas_call(
        prepare_kernel,
        grid=(3, NR // rows),
        in_specs=[pl.BlockSpec((1, rows, NR), lambda c, i: (c, i, 0))],
        out_specs=(spec, spec),
        out_shape=(shape, shape),
        cost_estimate=pl.CostEstimate(flops=10 * 3 * NR * NR, bytes_accessed=2 * 3 * NR * NR * 4, transcendentals=0),
        compiler_params=pltpu.CompilerParams(vmem_limit_bytes=10 * MIB),
        name="prepare",
    )(radial_inverse)


def solve_kernel(per, *refs):
    pieces, hi_ref, lo_ref, outs, lhs, result = refs[:8], refs[8], refs[9], refs[10:18], refs[18], refs[19]
    rows = 8 * per
    c = pl.program_id(0)
    for d, owner in enumerate(peers(-1)):
        block = pieces[d][c].reshape(rows, 128)
        hi = block.astype(jnp.bfloat16)
        at = pl.ds(pl.multiple_of(owner * 128, 128), 128)
        lhs[0:rows, at] = hi
        lhs[rows:, at] = (block - hi.astype(jnp.float32)).astype(jnp.bfloat16)
    for n in range(NR // 256):
        cols = slice(n * 256, (n + 1) * 256)
        both = jnp.dot(lhs[...], hi_ref[0, :, cols], preferred_element_type=jnp.float32)
        cross = jnp.dot(lhs[0:rows], lo_ref[0, :, cols], preferred_element_type=jnp.float32)
        result[:, cols] = both[0:rows] + (both[rows:] + cross)
    for d, owner in enumerate(peers(1)):
        outs[d][c] = result[:, pl.ds(pl.multiple_of(owner * 128, 128), 128)].reshape(8, per, 128)


def solve(chunk, pieces, hi, lo):
    per = chunk[1]
    rows = 8 * per
    matrix = pl.BlockSpec((1, NR, NR), lambda c: (c, 0, 0))
    return pl.pallas_call(
        functools.partial(solve_kernel, per),
        grid=(3,),
        in_specs=[whole()] * 8 + [matrix, matrix],
        out_specs=[whole()] * 8,
        out_shape=[piece(per)] * 8,
        scratch_shapes=[pltpu.VMEM((2 * rows, NR), jnp.bfloat16), pltpu.VMEM((rows, NR), jnp.float32)],
        cost_estimate=pl.CostEstimate(flops=3 * 3 * 2 * rows * NR * NR, bytes_accessed=3 * NR * NR * 4 + 2 * 3 * rows * NR * 4, transcendentals=0),
        compiler_params=pltpu.CompilerParams(vmem_limit_bytes=24 * MIB),
        name="solve",
    )(*pieces, hi, lo)


def place_kernel(chunk, *refs):
    per = chunk[1]
    pieces, out, sems = refs[:8], refs[-2], refs[-1]
    copies = []
    for d, owner in enumerate(peers(-1)):
        row = pl.multiple_of(row_of(chunk, owner), 8)
        copies.append(pltpu.make_async_copy(pieces[d], out.at[:, :, pl.ds(row, per)], sems.at[d]))
    for copy in copies:
        copy.start()
    for copy in copies:
        copy.wait()


def place(chunk, pieces, out):
    extra = () if out is None else (out,)
    return pl.pallas_call(
        functools.partial(place_kernel, chunk),
        in_specs=[whole()] * 8 + [anywhere()] * len(extra),
        out_specs=anywhere(),
        out_shape=piece(LENGTH),
        scratch_shapes=[pltpu.SemaphoreType.DMA((8,))],
        input_output_aliases={8: 0} if extra else {},
        cost_estimate=pl.CostEstimate(flops=0, bytes_accessed=2 * 3 * 8 * 8 * chunk[1] * 128 * 4, transcendentals=0),
        compiler_params=pltpu.CompilerParams(vmem_limit_bytes=8 * MIB),
        name="place",
    )(*pieces, *extra)


def exchange(pieces):
    return [pieces[0]] + [lax.ppermute(p, "rad", pairs(*hop)) for p, hop in zip(pieces[1:], HOPS[1:])]


def per_device(velocity, radial_inverse):
    size = lax.axis_size("theta")
    up = [(i, (i + 1) % size) for i in range(size)]
    below = lax.ppermute(velocity[:, :, LENGTH - 8 :], "theta", up)
    above = lax.ppermute(velocity[:, :, :8], "theta", [(b, a) for a, b in up])
    lane = lax.axis_index("rad") * 128 + jnp.arange(128)
    radius = 1.0 + (lane.astype(jnp.float32) + 0.5) / NR
    c_out = (viscous / 12.0) / radius
    coef = jnp.stack([radius - 30.0 * c_out, c_out] + [radius] * 6)
    hi, lo = prepare(radial_inverse)
    arrived = [exchange(stencil(chunk, velocity, below, above, coef)) for chunk in CHUNKS]
    back = [exchange(solve(chunk, pieces, hi, lo)) for chunk, pieces in zip(CHUNKS, arrived)]
    out = None
    for chunk, pieces in zip(CHUNKS, back):
        out = place(chunk, pieces, out)
    return out


def solution(mesh):
    return jax.shard_map(
        per_device,
        mesh=mesh,
        in_specs=(P(None, None, "theta", "rad"), P()),
        out_specs=P(None, None, "theta", "rad"),
        check_vma=False,
    )
```

```python
import functools
import jax
import jax.numpy as jnp
from jax import lax
from jax.experimental import pallas as pl
from jax.experimental.pallas import tpu as pltpu
from jax.sharding import PartitionSpec as P

NR = 1024
courant = 0.25
viscous = 0.05
LENGTH = 512
HOPS = ((0, 0), (2, 1), (2, 0), (0, 1), (1, 1), (3, 0), (3, 1), (1, 0))
GROUPS = ((1,), (2, 3), (4, 5), (6, 7, 0))
CHUNKS = ((128, 32, False), (0, 32, True))
MIB = 1 << 20


def whole():
    return pl.BlockSpec(memory_space=pltpu.VMEM)


def in_hbm():
    return pl.BlockSpec(memory_space=pltpu.HBM)


def piece(per):
    return jax.ShapeDtypeStruct((3, 8, per, 128), jnp.float32)


def peers(sign):
    me = lax.axis_index("rad")
    x, z = me // 2, me % 2
    return [lax.rem(x + (4 + sign * dx) % 4, 4) * 2 + (z + dz) % 2 for dx, dz in HOPS]


def pairs(dx, dz):
    return [(x * 2 + z, (x + dx) % 4 * 2 + (z + dz) % 2) for x in range(4) for z in range(2)]


def row_of(chunk, owner):
    first, per, ends = chunk
    if ends:
        return owner * per + jnp.where(owner >= 4, LENGTH - 8 * per, 0)
    return first + owner * per


def regroup(around, per, c, c_mid, c_out, swirl):
    m2, m1, mid, p1, p2 = (around[c][8 + k : 8 + k + per] for k in range(-2, 3))
    along = 8.0 * (p1 - m1) - (p2 - m2)
    outer = 16.0 * (p1 + m1) - (p2 + m2)
    return mid * c_mid - swirl * along + outer * c_out


def inner_kernel(chunk, group, velocity, coef, *refs):
    first, per, _ = chunk
    outs, window, sems = refs[: len(group)], refs[-2], refs[-1]
    owners = peers(1)

    def copy(n):
        row = pl.multiple_of(first - 8 + owners[group[n]] * per, 8)
        return pltpu.make_async_copy(velocity.at[:, :, pl.ds(row, per + 16)], window.at[n], sems.at[n])

    for n in range(len(group)):
        copy(n).start()
    for n in range(len(group)):
        copy(n).wait()

        @pl.loop(0, 8)
        def _(z):
            c_mid = coef[0:1, :]
            c_out = coef[1:2, :]
            around = [window[n, c, z] for c in range(3)]
            swirl = around[1][8 : 8 + per] * (courant / 12.0)
            for c in range(3):
                outs[n][c, z] = regroup(around, per, c, c_mid, c_out, swirl)


def ends_kernel(chunk, group, velocity, below, above, coef, *refs):
    _, per, _ = chunk
    outs, ext, sems = refs[: len(group)], refs[-2], refs[-1]
    half = 4 * per
    owners = peers(1)

    def copies(z):
        line = velocity.at[:, z]
        to = ext.at[:, z]
        return [
            pltpu.make_async_copy(below.at[:, z], to.at[:, pl.ds(0, 8)], sems.at[z, 0]),
            pltpu.make_async_copy(line.at[:, pl.ds(0, half + 8)], to.at[:, pl.ds(8, half + 8)], sems.at[z, 1]),
            pltpu.make_async_copy(line.at[:, pl.ds(LENGTH - half - 8, half + 8)], to.at[:, pl.ds(half + 16, half + 8)], sems.at[z, 2]),
            pltpu.make_async_copy(above.at[:, z], to.at[:, pl.ds(2 * half + 24, 8)], sems.at[z, 3]),
        ]

    for z in range(8):
        for copy in copies(z):
            copy.start()

    @pl.loop(0, 8)
    def _(z):
        for copy in copies(z):
            copy.wait()
        c_mid = coef[0:1, :]
        c_out = coef[1:2, :]
        for n, d in enumerate(group):
            start = pl.multiple_of(owners[d] * per + jnp.where(owners[d] >= 4, 16, 0), 8)
            around = [ext[c, z, pl.ds(start, per + 16), :] for c in range(3)]
            swirl = around[1][8 : 8 + per] * (courant / 12.0)
            for c in range(3):
                outs[n][c, z] = regroup(around, per, c, c_mid, c_out, swirl)


def stencil(chunk, group, velocity, below, above, coef):
    _, per, ends = chunk
    if ends:
        halos = (below, above)
        scratch = pltpu.VMEM((3, 8, 8 * per + 32, 128), jnp.float32)
        sems = pltpu.SemaphoreType.DMA((8, 4))
    else:
        halos = ()
        scratch = pltpu.VMEM((len(group), 3, 8, per + 16, 128), jnp.float32)
        sems = pltpu.SemaphoreType.DMA((len(group),))
    points = len(group) * 3 * 8 * per * 128
    return pl.pallas_call(
        functools.partial(ends_kernel if ends else inner_kernel, chunk, group),
        in_specs=[in_hbm()] + [whole()] * len(halos) + [whole()],
        out_specs=[whole()] * len(group),
        out_shape=[piece(per)] * len(group),
        scratch_shapes=[scratch, sems],
        cost_estimate=pl.CostEstimate(flops=points * 13, bytes_accessed=2 * points * 4, transcendentals=0),
        compiler_params=pltpu.CompilerParams(vmem_limit_bytes=12 * MIB),
        name="stencil",
    )(pltpu.with_memory_space_constraint(velocity, pltpu.HBM), *halos, coef)


def prepare_kernel(m_ref, hi_ref, lo_ref):
    rows = m_ref.shape[1]
    at = pl.program_id(1) * rows
    index = at + lax.broadcasted_iota(jnp.int32, (rows, 128), 0)
    scale = 1.0 / (1.0 + (index.astype(jnp.float32) + 0.5) / NR)
    for k in range(NR // 128):
        block = m_ref[0, :, k * 128 : (k + 1) * 128] * scale
        turned = block.T
        hi = turned.astype(jnp.bfloat16)
        hi_ref[0, k * 128 : (k + 1) * 128, :] = hi
        lo_ref[0, k * 128 : (k + 1) * 128, :] = (turned - hi.astype(jnp.float32)).astype(jnp.bfloat16)


def prepare(radial_inverse):
    rows = 256
    spec = pl.BlockSpec((1, NR, rows), lambda c, i: (c, 0, i))
    shape = jax.ShapeDtypeStruct((3, NR, NR), jnp.bfloat16)
    return pl.pallas_call(
        prepare_kernel,
        grid=(3, NR // rows),
        in_specs=[pl.BlockSpec((1, rows, NR), lambda c, i: (c, i, 0))],
        out_specs=(spec, spec),
        out_shape=(shape, shape),
        cost_estimate=pl.CostEstimate(flops=10 * 3 * NR * NR, bytes_accessed=2 * 3 * NR * NR * 4, transcendentals=0),
        compiler_params=pltpu.CompilerParams(vmem_limit_bytes=10 * MIB),
        name="prepare",
    )(pltpu.with_memory_space_constraint(radial_inverse, pltpu.HBM))


def solve_kernel(per, *refs):
    pieces, hi_ref, lo_ref, outs, lhs, result = refs[:8], refs[8], refs[9], refs[10:18], refs[18], refs[19]
    rows = 8 * per
    c = pl.program_id(0)
    for d, owner in enumerate(peers(-1)):
        block = pieces[d][c].reshape(rows, 128)
        hi = block.astype(jnp.bfloat16)
        at = pl.ds(pl.multiple_of(owner * 128, 128), 128)
        lhs[0:rows, at] = hi
        lhs[rows:, at] = (block - hi.astype(jnp.float32)).astype(jnp.bfloat16)
    for n in range(NR // 256):
        cols = slice(n * 256, (n + 1) * 256)
        both = jnp.dot(lhs[...], hi_ref[0, :, cols], preferred_element_type=jnp.float32)
        cross = jnp.dot(lhs[0:rows], lo_ref[0, :, cols], preferred_element_type=jnp.float32)
        result[:, cols] = both[0:rows] + (both[rows:] + cross)
    for d, owner in enumerate(peers(1)):
        outs[d][c] = result[:, pl.ds(pl.multiple_of(owner * 128, 128), 128)].reshape(8, per, 128)


def solve(chunk, pieces, hi, lo):
    per = chunk[1]
    rows = 8 * per
    matrix = pl.BlockSpec((1, NR, NR), lambda c: (c, 0, 0))
    return pl.pallas_call(
        functools.partial(solve_kernel, per),
        grid=(3,),
        in_specs=[whole()] * 8 + [matrix, matrix],
        out_specs=[whole()] * 8,
        out_shape=[piece(per)] * 8,
        scratch_shapes=[pltpu.VMEM((2 * rows, NR), jnp.bfloat16), pltpu.VMEM((rows, NR), jnp.float32)],
        cost_estimate=pl.CostEstimate(flops=3 * 3 * 2 * rows * NR * NR, bytes_accessed=3 * NR * NR * 4 + 2 * 3 * rows * NR * 4, transcendentals=0),
        compiler_params=pltpu.CompilerParams(vmem_limit_bytes=24 * MIB),
        name="solve",
    )(*pieces, hi, lo)


def place_kernel(chunk, group, *refs):
    per = chunk[1]
    pieces, out, sems = refs[: len(group)], refs[-2], refs[-1]
    owners = peers(-1)
    copies = []
    for n, d in enumerate(group):
        row = pl.multiple_of(row_of(chunk, owners[d]), 8)
        copies.append(pltpu.make_async_copy(pieces[n], out.at[:, :, pl.ds(row, per)], sems.at[n]))
    for copy in copies:
        copy.start()
    for copy in copies:
        copy.wait()


def place(chunk, group, pieces, out):
    extra = () if out is None else (out,)
    return pl.pallas_call(
        functools.partial(place_kernel, chunk, group),
        in_specs=[whole()] * len(group) + [in_hbm()] * len(extra),
        out_specs=in_hbm(),
        out_shape=piece(LENGTH),
        scratch_shapes=[pltpu.SemaphoreType.DMA((len(group),))],
        input_output_aliases={len(group): 0} if extra else {},
        cost_estimate=pl.CostEstimate(flops=0, bytes_accessed=2 * 3 * 8 * len(group) * chunk[1] * 128 * 4, transcendentals=0),
        compiler_params=pltpu.CompilerParams(vmem_limit_bytes=4 * MIB),
        name="place",
    )(*[pieces[d] for d in group], *extra)


def exchange(pieces):
    return [pieces[0]] + [lax.ppermute(p, "rad", pairs(*hop)) for p, hop in zip(pieces[1:], HOPS[1:])]


def per_device(velocity, radial_inverse):
    size = lax.axis_size("theta")
    up = [(i, (i + 1) % size) for i in range(size)]
    below = lax.ppermute(velocity[:, :, LENGTH - 8 :], "theta", up)
    above = lax.ppermute(velocity[:, :, :8], "theta", [(b, a) for a, b in up])
    lane = lax.axis_index("rad") * 128 + jnp.arange(128)
    radius = 1.0 + (lane.astype(jnp.float32) + 0.5) / NR
    c_out = (viscous / 12.0) / radius
    coef = jnp.stack([radius - 30.0 * c_out, c_out] + [radius] * 6)
    weighted = []
    for chunk in CHUNKS:
        pieces = [None] * 8
        for group in (tuple(range(8)),) if chunk[2] else GROUPS:
            for d, made in zip(group, stencil(chunk, group, velocity, below, above, coef)):
                pieces[d] = made
        weighted.append(pieces)
    radial_inverse, weighted[-1][0] = lax.optimization_barrier((radial_inverse, weighted[-1][0]))
    arrived = [exchange(pieces) for pieces in weighted]
    hi, lo = prepare(radial_inverse)
    back = [exchange(solve(chunk, pieces, hi, lo)) for chunk, pieces in zip(CHUNKS, arrived)]
    out = place(CHUNKS[0], range(8), back[0], None)
    out = place(CHUNKS[1], (0, 1, 2, 3, 4), back[1], out)
    return place(CHUNKS[1], (5, 6, 7), back[1], out)


def solution(mesh):
    return jax.shard_map(
        per_device,
        mesh=mesh,
        in_specs=(P(None, None, "theta", "rad"), P()),
        out_specs=P(None, None, "theta", "rad"),
        check_vma=False,
    )
```

```python
import functools
import jax
import jax.numpy as jnp
from jax import lax
from jax.experimental import pallas as pl
from jax.experimental.pallas import tpu as pltpu
from jax.sharding import PartitionSpec as P

NR = 1024
courant = 0.25
viscous = 0.05
LENGTH = 512
ORDERS = ((5, 4, 3, 1, 6, 7, 2, 0), (5, 4, 3, 1, 6, 7, 2, 0), (5, 4, 3, 1, 6, 7, 2, 0), (5, 4, 3, 1, 6, 7, 2, 0))
SPLIT = (1, 3, 5, 8)
LAST = (5, 8)
CHUNKS = ((128, 32, False), (0, 32, True))
MIB = 1 << 20


def whole():
    return pl.BlockSpec(memory_space=pltpu.VMEM)


def in_hbm():
    return pl.BlockSpec(memory_space=pltpu.HBM)


def piece(per):
    return jax.ShapeDtypeStruct((3, 8, per, 128), jnp.float32)


def owner_of(d):
    return lax.axis_index("rad") ^ d


def row_of(chunk, owner):
    first, per, ends = chunk
    if ends:
        return owner * per + jnp.where(owner >= 4, LENGTH - 8 * per, 0)
    return first + owner * per


def regroup(around, per, c, c_mid, c_out, swirl):
    m2, m1, mid, p1, p2 = (around[c][8 + k : 8 + k + per] for k in range(-2, 3))
    along = 8.0 * (p1 - m1) - (p2 - m2)
    outer = 16.0 * (p1 + m1) - (p2 + m2)
    return mid * c_mid - swirl * along + outer * c_out


def inner_kernel(chunk, group, velocity, coef, *refs):
    first, per, _ = chunk
    outs, window, sems = refs[: len(group)], refs[-2], refs[-1]

    def copy(n):
        row = pl.multiple_of(first - 8 + owner_of(group[n]) * per, 8)
        return pltpu.make_async_copy(velocity.at[:, :, pl.ds(row, per + 16)], window.at[n], sems.at[n])

    for n in range(len(group)):
        copy(n).start()
    for n in range(len(group)):
        copy(n).wait()

        @pl.loop(0, 8)
        def _(z):
            c_mid = coef[0:1, :]
            c_out = coef[1:2, :]
            around = [window[n, c, z] for c in range(3)]
            swirl = around[1][8 : 8 + per] * (courant / 12.0)
            for c in range(3):
                outs[n][c, z] = regroup(around, per, c, c_mid, c_out, swirl)


def ends_kernel(chunk, group, velocity, below, above, coef, *refs):
    _, per, _ = chunk
    outs, ext, sems = refs[: len(group)], refs[-2], refs[-1]
    half = 4 * per

    def copies(z):
        line = velocity.at[:, z]
        to = ext.at[:, z]
        return [
            pltpu.make_async_copy(below.at[:, z], to.at[:, pl.ds(0, 8)], sems.at[z, 0]),
            pltpu.make_async_copy(line.at[:, pl.ds(0, half + 8)], to.at[:, pl.ds(8, half + 8)], sems.at[z, 1]),
            pltpu.make_async_copy(line.at[:, pl.ds(LENGTH - half - 8, half + 8)], to.at[:, pl.ds(half + 16, half + 8)], sems.at[z, 2]),
            pltpu.make_async_copy(above.at[:, z], to.at[:, pl.ds(2 * half + 24, 8)], sems.at[z, 3]),
        ]

    for z in range(8):
        for copy in copies(z):
            copy.start()

    @pl.loop(0, 8)
    def _(z):
        for copy in copies(z):
            copy.wait()
        c_mid = coef[0:1, :]
        c_out = coef[1:2, :]
        for n, d in enumerate(group):
            owner = owner_of(d)
            start = pl.multiple_of(owner * per + jnp.where(owner >= 4, 16, 0), 8)
            around = [ext[c, z, pl.ds(start, per + 16), :] for c in range(3)]
            swirl = around[1][8 : 8 + per] * (courant / 12.0)
            for c in range(3):
                outs[n][c, z] = regroup(around, per, c, c_mid, c_out, swirl)


def stencil(chunk, group, velocity, below, above, coef):
    _, per, ends = chunk
    if ends:
        halos = (below, above)
        scratch = pltpu.VMEM((3, 8, 8 * per + 32, 128), jnp.float32)
        sems = pltpu.SemaphoreType.DMA((8, 4))
    else:
        halos = ()
        scratch = pltpu.VMEM((len(group), 3, 8, per + 16, 128), jnp.float32)
        sems = pltpu.SemaphoreType.DMA((len(group),))
    points = len(group) * 3 * 8 * per * 128
    return pl.pallas_call(
        functools.partial(ends_kernel if ends else inner_kernel, chunk, group),
        in_specs=[in_hbm()] + [whole()] * len(halos) + [whole()],
        out_specs=[whole()] * len(group),
        out_shape=[piece(per)] * len(group),
        scratch_shapes=[scratch, sems],
        cost_estimate=pl.CostEstimate(flops=points * 13, bytes_accessed=2 * points * 4, transcendentals=0),
        compiler_params=pltpu.CompilerParams(vmem_limit_bytes=12 * MIB),
        name="stencil",
    )(pltpu.with_memory_space_constraint(velocity, pltpu.HBM), *halos, coef)


def prepare_kernel(m_ref, hi_ref, lo_ref):
    rows = m_ref.shape[1]
    at = pl.program_id(1) * rows
    index = at + lax.broadcasted_iota(jnp.int32, (rows, 128), 0)
    scale = 1.0 / (1.0 + (index.astype(jnp.float32) + 0.5) / NR)
    for k in range(NR // 128):
        block = m_ref[0, :, k * 128 : (k + 1) * 128] * scale
        turned = block.T
        hi = turned.astype(jnp.bfloat16)
        hi_ref[0, k * 128 : (k + 1) * 128, :] = hi
        lo_ref[0, k * 128 : (k + 1) * 128, :] = (turned - hi.astype(jnp.float32)).astype(jnp.bfloat16)


def prepare(radial_inverse):
    rows = 256
    spec = pl.BlockSpec((1, NR, rows), lambda c, i: (c, 0, i))
    shape = jax.ShapeDtypeStruct((3, NR, NR), jnp.bfloat16)
    return pl.pallas_call(
        prepare_kernel,
        grid=(3, NR // rows),
        in_specs=[pl.BlockSpec((1, rows, NR), lambda c, i: (c, i, 0))],
        out_specs=(spec, spec),
        out_shape=(shape, shape),
        cost_estimate=pl.CostEstimate(flops=10 * 3 * NR * NR, bytes_accessed=2 * 3 * NR * NR * 4, transcendentals=0),
        compiler_params=pltpu.CompilerParams(vmem_limit_bytes=10 * MIB),
        name="prepare",
    )(pltpu.with_memory_space_constraint(radial_inverse, pltpu.HBM))


def solve_kernel(per, sources, targets, *refs):
    pieces, hi_ref, lo_ref, outs, lhs, result = refs[:8], refs[8], refs[9], refs[10:18], refs[18], refs[19]
    rows = 8 * per
    c = pl.program_id(0)
    for n, d in enumerate(sources):
        block = pieces[n][c].reshape(rows, 128)
        hi = block.astype(jnp.bfloat16)
        at = pl.ds(pl.multiple_of(owner_of(d) * 128, 128), 128)
        lhs[0:rows, at] = hi
        lhs[rows:, at] = (block - hi.astype(jnp.float32)).astype(jnp.bfloat16)
    for n in range(NR // 256):
        cols = slice(n * 256, (n + 1) * 256)
        both = jnp.dot(lhs[...], hi_ref[0, :, cols], preferred_element_type=jnp.float32)
        cross = jnp.dot(lhs[0:rows], lo_ref[0, :, cols], preferred_element_type=jnp.float32)
        result[:, cols] = both[0:rows] + (both[rows:] + cross)
    for n, d in enumerate(targets):
        outs[n][c] = result[:, pl.ds(pl.multiple_of(owner_of(d) * 128, 128), 128)].reshape(8, per, 128)


def solve(chunk, sources, targets, pieces, hi, lo):
    per = chunk[1]
    rows = 8 * per
    matrix = pl.BlockSpec((1, NR, NR), lambda c: (c, 0, 0))
    return pl.pallas_call(
        functools.partial(solve_kernel, per, sources, targets),
        grid=(3,),
        in_specs=[whole()] * 8 + [matrix, matrix],
        out_specs=[whole()] * 8,
        out_shape=[piece(per)] * 8,
        scratch_shapes=[pltpu.VMEM((2 * rows, NR), jnp.bfloat16), pltpu.VMEM((rows, NR), jnp.float32)],
        cost_estimate=pl.CostEstimate(flops=3 * 3 * 2 * rows * NR * NR, bytes_accessed=3 * NR * NR * 4 + 2 * 3 * rows * NR * 4, transcendentals=0),
        compiler_params=pltpu.CompilerParams(vmem_limit_bytes=24 * MIB),
        name="solve",
    )(*pieces, hi, lo)


def place_kernel(chunk, group, *refs):
    per = chunk[1]
    pieces, out, sems = refs[: len(group)], refs[-2], refs[-1]
    copies = []
    for n, d in enumerate(group):
        row = pl.multiple_of(row_of(chunk, owner_of(d)), 8)
        copies.append(pltpu.make_async_copy(pieces[n], out.at[:, :, pl.ds(row, per)], sems.at[n]))
    for copy in copies:
        copy.start()
    for copy in copies:
        copy.wait()


def place(chunk, group, pieces, out):
    extra = () if out is None else (out,)
    return pl.pallas_call(
        functools.partial(place_kernel, chunk, group),
        in_specs=[whole()] * len(group) + [in_hbm()] * len(extra),
        out_specs=in_hbm(),
        out_shape=piece(LENGTH),
        scratch_shapes=[pltpu.SemaphoreType.DMA((len(group),))],
        input_output_aliases={len(group): 0} if extra else {},
        cost_estimate=pl.CostEstimate(flops=0, bytes_accessed=2 * 3 * 8 * len(group) * chunk[1] * 128 * 4, transcendentals=0),
        compiler_params=pltpu.CompilerParams(vmem_limit_bytes=4 * MIB),
        name="place",
    )(*pieces, *extra)


def exchange(pieces, order):
    return [p if d == 0 else lax.ppermute(p, "rad", [(i, i ^ d) for i in range(8)]) for p, d in zip(pieces, order)]


def per_device(velocity, radial_inverse):
    size = lax.axis_size("theta")
    up = [(i, (i + 1) % size) for i in range(size)]
    below = lax.ppermute(velocity[:, :, LENGTH - 8 :], "theta", up)
    above = lax.ppermute(velocity[:, :, :8], "theta", [(b, a) for a, b in up])
    lane = lax.axis_index("rad") * 128 + jnp.arange(128)
    radius = 1.0 + (lane.astype(jnp.float32) + 0.5) / NR
    c_out = (viscous / 12.0) / radius
    coef = jnp.stack([radius - 30.0 * c_out, c_out] + [radius] * 6)
    count = len(CHUNKS)
    weighted = []
    for chunk, order in zip(CHUNKS, ORDERS):
        pieces = []
        for stop in SPLIT if chunk is CHUNKS[0] else (8,):
            group = order[len(pieces) : stop]
            pieces += stencil(chunk, group, velocity, below, above, coef)
        weighted.append(pieces)
    radial_inverse, weighted[-1][-1] = lax.optimization_barrier((radial_inverse, weighted[-1][-1]))
    arrived = [exchange(pieces, order) for pieces, order in zip(weighted, ORDERS)]
    hi, lo = prepare(radial_inverse)
    out = None
    back = []
    for chunk, pieces, order, target in zip(CHUNKS, arrived, ORDERS, ORDERS[count:]):
        back.append(exchange(solve(chunk, order, target, pieces, hi, lo), target))
    for chunk, pieces, order in zip(CHUNKS, back, ORDERS[count:]):
        start = 0
        for stop in LAST if chunk is CHUNKS[-1] else (8,):
            out = place(chunk, order[start:stop], pieces[start:stop], out)
            start = stop
    return out


def solution(mesh):
    return jax.shard_map(
        per_device,
        mesh=mesh,
        in_specs=(P(None, None, "theta", "rad"), P()),
        out_specs=P(None, None, "theta", "rad"),
        check_vma=False,
    )
```

```python
import functools
import jax
import jax.numpy as jnp
from jax import lax
from jax.experimental import pallas as pl
from jax.experimental.pallas import tpu as pltpu
from jax.sharding import PartitionSpec as P

NR = 1024
courant = 0.25
viscous = 0.05
LENGTH = 512
ORDERS = ((5, 4, 3, 1, 6, 7, 2, 0), (5, 4, 3, 1, 6, 7, 2, 0), (5, 4, 3, 1, 6, 7, 2, 0), (0, 5, 4, 3, 1, 6, 7, 2))
SPLIT = (1, 3, 5, 8)
LAST = (6, 8)
CHUNKS = ((96, 40, False), (0, 24, True))
MIB = 1 << 20


def whole():
    return pl.BlockSpec(memory_space=pltpu.VMEM)


def in_hbm():
    return pl.BlockSpec(memory_space=pltpu.HBM)


def piece(per):
    return jax.ShapeDtypeStruct((3, 8, per, 128), jnp.float32)


def owner_of(d):
    return lax.axis_index("rad") ^ d


def row_of(chunk, owner):
    first, per, ends = chunk
    if ends:
        return owner * per + jnp.where(owner >= 4, LENGTH - 8 * per, 0)
    return first + owner * per


def regroup(around, per, c, c_mid, c_out, swirl):
    m2, m1, mid, p1, p2 = (around[c][8 + k : 8 + k + per] for k in range(-2, 3))
    along = 8.0 * (p1 - m1) - (p2 - m2)
    outer = 16.0 * (p1 + m1) - (p2 + m2)
    return mid * c_mid - swirl * along + outer * c_out


def inner_kernel(chunk, group, velocity, coef, *refs):
    first, per, _ = chunk
    outs, window, sems = refs[: len(group)], refs[-2], refs[-1]

    def copy(n, z):
        row = pl.multiple_of(first - 8 + owner_of(group[n]) * per, 8)
        return pltpu.make_async_copy(velocity.at[:, z, pl.ds(row, per + 16)], window.at[n, :, z], sems.at[n, z])

    for n in range(len(group)):
        for z in range(8):
            copy(n, z).start()
    for n in range(len(group)):

        @pl.loop(0, 8)
        def _(z):
            copy(n, z).wait()
            c_mid = coef[0:1, :]
            c_out = coef[1:2, :]
            around = [window[n, c, z] for c in range(3)]
            swirl = around[1][8 : 8 + per] * (courant / 12.0)
            for c in range(3):
                outs[n][c, z] = regroup(around, per, c, c_mid, c_out, swirl)


def ends_kernel(chunk, group, velocity, below, above, coef, *refs):
    _, per, _ = chunk
    outs, ext, sems = refs[: len(group)], refs[-2], refs[-1]
    half = 4 * per

    def copies(z):
        line = velocity.at[:, z]
        to = ext.at[:, z]
        return [
            pltpu.make_async_copy(below.at[:, z], to.at[:, pl.ds(0, 8)], sems.at[z, 0]),
            pltpu.make_async_copy(line.at[:, pl.ds(0, half + 8)], to.at[:, pl.ds(8, half + 8)], sems.at[z, 1]),
            pltpu.make_async_copy(line.at[:, pl.ds(LENGTH - half - 8, half + 8)], to.at[:, pl.ds(half + 16, half + 8)], sems.at[z, 2]),
            pltpu.make_async_copy(above.at[:, z], to.at[:, pl.ds(2 * half + 24, 8)], sems.at[z, 3]),
        ]

    for z in range(8):
        for copy in copies(z):
            copy.start()

    @pl.loop(0, 8)
    def _(z):
        for copy in copies(z):
            copy.wait()
        c_mid = coef[0:1, :]
        c_out = coef[1:2, :]
        for n, d in enumerate(group):
            owner = owner_of(d)
            start = pl.multiple_of(owner * per + jnp.where(owner >= 4, 16, 0), 8)
            around = [ext[c, z, pl.ds(start, per + 16), :] for c in range(3)]
            swirl = around[1][8 : 8 + per] * (courant / 12.0)
            for c in range(3):
                outs[n][c, z] = regroup(around, per, c, c_mid, c_out, swirl)


def stencil(chunk, group, velocity, below, above, coef):
    _, per, ends = chunk
    if ends:
        halos = (below, above)
        scratch = pltpu.VMEM((3, 8, 8 * per + 32, 128), jnp.float32)
        sems = pltpu.SemaphoreType.DMA((8, 4))
    else:
        halos = ()
        scratch = pltpu.VMEM((len(group), 3, 8, per + 16, 128), jnp.float32)
        sems = pltpu.SemaphoreType.DMA((len(group), 8))
    points = len(group) * 3 * 8 * per * 128
    return pl.pallas_call(
        functools.partial(ends_kernel if ends else inner_kernel, chunk, group),
        in_specs=[in_hbm()] + [whole()] * len(halos) + [whole()],
        out_specs=[whole()] * len(group),
        out_shape=[piece(per)] * len(group),
        scratch_shapes=[scratch, sems],
        cost_estimate=pl.CostEstimate(flops=points * 13, bytes_accessed=2 * points * 4, transcendentals=0),
        compiler_params=pltpu.CompilerParams(vmem_limit_bytes=12 * MIB),
        name="stencil",
    )(pltpu.with_memory_space_constraint(velocity, pltpu.HBM), *halos, coef)


def prepare_kernel(m_ref, hi_ref, lo_ref):
    rows = m_ref.shape[1]
    at = pl.program_id(1) * rows
    index = at + lax.broadcasted_iota(jnp.int32, (rows, 128), 0)
    scale = 1.0 / (1.0 + (index.astype(jnp.float32) + 0.5) / NR)
    for k in range(NR // 128):
        block = m_ref[0, :, k * 128 : (k + 1) * 128] * scale
        turned = block.T
        hi = turned.astype(jnp.bfloat16)
        hi_ref[0, k * 128 : (k + 1) * 128, :] = hi
        lo_ref[0, k * 128 : (k + 1) * 128, :] = (turned - hi.astype(jnp.float32)).astype(jnp.bfloat16)


def prepare(radial_inverse):
    rows = 256
    spec = pl.BlockSpec((1, NR, rows), lambda c, i: (c, 0, i))
    shape = jax.ShapeDtypeStruct((3, NR, NR), jnp.bfloat16)
    return pl.pallas_call(
        prepare_kernel,
        grid=(3, NR // rows),
        in_specs=[pl.BlockSpec((1, rows, NR), lambda c, i: (c, i, 0))],
        out_specs=(spec, spec),
        out_shape=(shape, shape),
        cost_estimate=pl.CostEstimate(flops=10 * 3 * NR * NR, bytes_accessed=2 * 3 * NR * NR * 4, transcendentals=0),
        compiler_params=pltpu.CompilerParams(vmem_limit_bytes=10 * MIB),
        name="prepare",
    )(pltpu.with_memory_space_constraint(radial_inverse, pltpu.HBM))


def solve_kernel(per, sources, targets, *refs):
    pieces, hi_ref, lo_ref, outs, lhs, result = refs[:8], refs[8], refs[9], refs[10:18], refs[18], refs[19]
    rows = 8 * per
    c = pl.program_id(0)
    for n, d in enumerate(sources):
        block = pieces[n][c].reshape(rows, 128)
        hi = block.astype(jnp.bfloat16)
        at = pl.ds(pl.multiple_of(owner_of(d) * 128, 128), 128)
        lhs[0:rows, at] = hi
        lhs[rows:, at] = (block - hi.astype(jnp.float32)).astype(jnp.bfloat16)
    for n in range(NR // 256):
        cols = slice(n * 256, (n + 1) * 256)
        both = jnp.dot(lhs[...], hi_ref[0, :, cols], preferred_element_type=jnp.float32)
        cross = jnp.dot(lhs[0:rows], lo_ref[0, :, cols], preferred_element_type=jnp.float32)
        result[:, cols] = both[0:rows] + (both[rows:] + cross)
    for n, d in enumerate(targets):
        outs[n][c] = result[:, pl.ds(pl.multiple_of(owner_of(d) * 128, 128), 128)].reshape(8, per, 128)


def solve(chunk, sources, targets, pieces, hi, lo):
    per = chunk[1]
    rows = 8 * per
    matrix = pl.BlockSpec((1, NR, NR), lambda c: (c, 0, 0))
    return pl.pallas_call(
        functools.partial(solve_kernel, per, sources, targets),
        grid=(3,),
        in_specs=[whole()] * 8 + [matrix, matrix],
        out_specs=[whole()] * 8,
        out_shape=[piece(per)] * 8,
        scratch_shapes=[pltpu.VMEM((2 * rows, NR), jnp.bfloat16), pltpu.VMEM((rows, NR), jnp.float32)],
        cost_estimate=pl.CostEstimate(flops=3 * 3 * 2 * rows * NR * NR, bytes_accessed=3 * NR * NR * 4 + 2 * 3 * rows * NR * 4, transcendentals=0),
        compiler_params=pltpu.CompilerParams(vmem_limit_bytes=24 * MIB),
        name="solve",
    )(*pieces, hi, lo)


def place_kernel(chunk, group, *refs):
    per = chunk[1]
    pieces, out, sems = refs[: len(group)], refs[-2], refs[-1]
    copies = []
    for n, d in enumerate(group):
        row = pl.multiple_of(row_of(chunk, owner_of(d)), 8)
        for c in range(3):
            copies.append(pltpu.make_async_copy(pieces[n].at[c], out.at[c, :, pl.ds(row, per)], sems.at[n, c]))
    for copy in copies:
        copy.start()
    for copy in copies:
        copy.wait()


def place(chunk, group, pieces, out):
    extra = () if out is None else (out,)
    return pl.pallas_call(
        functools.partial(place_kernel, chunk, group),
        in_specs=[whole()] * len(group) + [in_hbm()] * len(extra),
        out_specs=in_hbm(),
        out_shape=piece(LENGTH),
        scratch_shapes=[pltpu.SemaphoreType.DMA((len(group), 3))],
        input_output_aliases={len(group): 0} if extra else {},
        cost_estimate=pl.CostEstimate(flops=0, bytes_accessed=2 * 3 * 8 * len(group) * chunk[1] * 128 * 4, transcendentals=0),
        compiler_params=pltpu.CompilerParams(vmem_limit_bytes=4 * MIB),
        name="place",
    )(*pieces, *extra)


def exchange(pieces, order):
    return [p if d == 0 else lax.ppermute(p, "rad", [(i, i ^ d) for i in range(8)]) for p, d in zip(pieces, order)]


def per_device(velocity, radial_inverse):
    size = lax.axis_size("theta")
    up = [(i, (i + 1) % size) for i in range(size)]
    below = lax.ppermute(velocity[:, :, LENGTH - 8 :], "theta", up)
    above = lax.ppermute(velocity[:, :, :8], "theta", [(b, a) for a, b in up])
    lane = lax.axis_index("rad") * 128 + jnp.arange(128)
    radius = 1.0 + (lane.astype(jnp.float32) + 0.5) / NR
    c_out = (viscous / 12.0) / radius
    coef = jnp.stack([radius - 30.0 * c_out, c_out] + [radius] * 6)
    count = len(CHUNKS)
    weighted = []
    for chunk, order in zip(CHUNKS, ORDERS):
        pieces = []
        for stop in SPLIT if chunk is CHUNKS[0] else (8,):
            group = order[len(pieces) : stop]
            pieces += stencil(chunk, group, velocity, below, above, coef)
        weighted.append(pieces)
    radial_inverse, weighted[-1][-1] = lax.optimization_barrier((radial_inverse, weighted[-1][-1]))
    arrived = [exchange(pieces, order) for pieces, order in zip(weighted, ORDERS)]
    hi, lo = prepare(radial_inverse)
    out = None
    back = []
    for chunk, pieces, order, target in zip(CHUNKS, arrived, ORDERS, ORDERS[count:]):
        back.append(exchange(solve(chunk, order, target, pieces, hi, lo), target))
    for chunk, pieces, order in zip(CHUNKS, back, ORDERS[count:]):
        start = 0
        for stop in LAST if chunk is CHUNKS[-1] else (8,):
            out = place(chunk, order[start:stop], pieces[start:stop], out)
            start = stop
    return out


def solution(mesh):
    return jax.shard_map(
        per_device,
        mesh=mesh,
        in_specs=(P(None, None, "theta", "rad"), P()),
        out_specs=P(None, None, "theta", "rad"),
        check_vma=False,
    )
```

```python
import functools
import jax
import jax.numpy as jnp
from jax import lax
from jax.experimental import pallas as pl
from jax.experimental.pallas import tpu as pltpu
from jax.sharding import PartitionSpec as P

NR = 1024
courant = 0.25
viscous = 0.05
LENGTH = 512
ORDERS = ((5, 4, 3, 1, 6, 7, 2, 0), (5, 4, 3, 1, 6, 7, 2, 0), (5, 4, 3, 1, 6, 7, 2, 0), (0, 5, 4, 3, 1, 6, 2, 7))
SPLIT = (1, 3, 5, 8)
LAST = (7, 8)
CHUNKS = ((96, 40, False), (0, 24, True))
MIB = 1 << 20


def whole():
    return pl.BlockSpec(memory_space=pltpu.VMEM)


def in_hbm():
    return pl.BlockSpec(memory_space=pltpu.HBM)


def piece(per):
    return jax.ShapeDtypeStruct((3, 8, per, 128), jnp.float32)


def owner_of(d):
    return lax.axis_index("rad") ^ d


def row_of(chunk, owner):
    first, per, ends = chunk
    if ends:
        return owner * per + jnp.where(owner >= 4, LENGTH - 8 * per, 0)
    return first + owner * per


def regroup(around, per, c, c_mid, c_out, swirl):
    m2, m1, mid, p1, p2 = (around[c][8 + k : 8 + k + per] for k in range(-2, 3))
    along = 8.0 * (p1 - m1) - (p2 - m2)
    outer = 16.0 * (p1 + m1) - (p2 + m2)
    return mid * c_mid - swirl * along + outer * c_out


def inner_kernel(chunk, group, velocity, coef, *refs):
    first, per, _ = chunk
    outs, window, sems = refs[: len(group)], refs[-2], refs[-1]

    def copy(n, z):
        row = pl.multiple_of(first - 8 + owner_of(group[n]) * per, 8)
        return pltpu.make_async_copy(velocity.at[:, z, pl.ds(row, per + 16)], window.at[n, :, z], sems.at[n, z])

    for n in range(len(group)):
        for z in range(8):
            copy(n, z).start()
    for n in range(len(group)):

        @pl.loop(0, 8)
        def _(z):
            copy(n, z).wait()
            c_mid = coef[0:1, :]
            c_out = coef[1:2, :]
            around = [window[n, c, z] for c in range(3)]
            swirl = around[1][8 : 8 + per] * (courant / 12.0)
            for c in range(3):
                outs[n][c, z] = regroup(around, per, c, c_mid, c_out, swirl)


def ends_kernel(chunk, group, velocity, below, above, coef, *refs):
    _, per, _ = chunk
    outs, ext, sems = refs[: len(group)], refs[-2], refs[-1]
    half = 4 * per

    def copies(z):
        line = velocity.at[:, z]
        to = ext.at[:, z]
        return [
            pltpu.make_async_copy(below.at[:, z], to.at[:, pl.ds(0, 8)], sems.at[z, 0]),
            pltpu.make_async_copy(line.at[:, pl.ds(0, half + 8)], to.at[:, pl.ds(8, half + 8)], sems.at[z, 1]),
            pltpu.make_async_copy(line.at[:, pl.ds(LENGTH - half - 8, half + 8)], to.at[:, pl.ds(half + 16, half + 8)], sems.at[z, 2]),
            pltpu.make_async_copy(above.at[:, z], to.at[:, pl.ds(2 * half + 24, 8)], sems.at[z, 3]),
        ]

    for z in range(8):
        for copy in copies(z):
            copy.start()

    @pl.loop(0, 8)
    def _(z):
        for copy in copies(z):
            copy.wait()
        c_mid = coef[0:1, :]
        c_out = coef[1:2, :]
        for n, d in enumerate(group):
            owner = owner_of(d)
            start = pl.multiple_of(owner * per + jnp.where(owner >= 4, 16, 0), 8)
            around = [ext[c, z, pl.ds(start, per + 16), :] for c in range(3)]
            swirl = around[1][8 : 8 + per] * (courant / 12.0)
            for c in range(3):
                outs[n][c, z] = regroup(around, per, c, c_mid, c_out, swirl)


def stencil(chunk, group, velocity, below, above, coef):
    _, per, ends = chunk
    if ends:
        halos = (below, above)
        scratch = pltpu.VMEM((3, 8, 8 * per + 32, 128), jnp.float32)
        sems = pltpu.SemaphoreType.DMA((8, 4))
    else:
        halos = ()
        scratch = pltpu.VMEM((len(group), 3, 8, per + 16, 128), jnp.float32)
        sems = pltpu.SemaphoreType.DMA((len(group), 8))
    points = len(group) * 3 * 8 * per * 128
    return pl.pallas_call(
        functools.partial(ends_kernel if ends else inner_kernel, chunk, group),
        in_specs=[in_hbm()] + [whole()] * len(halos) + [whole()],
        out_specs=[whole()] * len(group),
        out_shape=[piece(per)] * len(group),
        scratch_shapes=[scratch, sems],
        cost_estimate=pl.CostEstimate(flops=points * 13, bytes_accessed=2 * points * 4, transcendentals=0),
        compiler_params=pltpu.CompilerParams(vmem_limit_bytes=12 * MIB),
        name="stencil",
    )(pltpu.with_memory_space_constraint(velocity, pltpu.HBM), *halos, coef)


def prepare_kernel(m_ref, hi_ref, lo_ref):
    rows = m_ref.shape[1]
    at = pl.program_id(1) * rows
    index = at + lax.broadcasted_iota(jnp.int32, (rows, 128), 0)
    scale = 1.0 / (1.0 + (index.astype(jnp.float32) + 0.5) / NR)
    for k in range(NR // 128):
        block = m_ref[0, :, k * 128 : (k + 1) * 128] * scale
        turned = block.T
        hi = turned.astype(jnp.bfloat16)
        hi_ref[0, k * 128 : (k + 1) * 128, :] = hi
        lo_ref[0, k * 128 : (k + 1) * 128, :] = (turned - hi.astype(jnp.float32)).astype(jnp.bfloat16)


def prepare(radial_inverse):
    rows = 256
    spec = pl.BlockSpec((1, NR, rows), lambda c, i: (c, 0, i))
    shape = jax.ShapeDtypeStruct((3, NR, NR), jnp.bfloat16)
    return pl.pallas_call(
        prepare_kernel,
        grid=(3, NR // rows),
        in_specs=[pl.BlockSpec((1, rows, NR), lambda c, i: (c, i, 0))],
        out_specs=(spec, spec),
        out_shape=(shape, shape),
        cost_estimate=pl.CostEstimate(flops=10 * 3 * NR * NR, bytes_accessed=2 * 3 * NR * NR * 4, transcendentals=0),
        compiler_params=pltpu.CompilerParams(vmem_limit_bytes=10 * MIB),
        name="prepare",
    )(pltpu.with_memory_space_constraint(radial_inverse, pltpu.HBM))


def solve_kernel(per, sources, targets, *refs):
    pieces, hi_ref, lo_ref, outs, lhs, result = refs[:8], refs[8], refs[9], refs[10:18], refs[18], refs[19]
    rows = 8 * per
    c = pl.program_id(0)
    for n, d in enumerate(sources):
        block = pieces[n][c].reshape(rows, 128)
        hi = block.astype(jnp.bfloat16)
        at = pl.ds(pl.multiple_of(owner_of(d) * 128, 128), 128)
        lhs[0:rows, at] = hi
        lhs[rows:, at] = (block - hi.astype(jnp.float32)).astype(jnp.bfloat16)
    for n in range(NR // 256):
        cols = slice(n * 256, (n + 1) * 256)
        both = jnp.dot(lhs[...], hi_ref[0, :, cols], preferred_element_type=jnp.float32)
        cross = jnp.dot(lhs[0:rows], lo_ref[0, :, cols], preferred_element_type=jnp.float32)
        result[:, cols] = both[0:rows] + (both[rows:] + cross)
    for n, d in enumerate(targets):
        outs[n][c] = result[:, pl.ds(pl.multiple_of(owner_of(d) * 128, 128), 128)].reshape(8, per, 128)


def solve(chunk, sources, targets, pieces, hi, lo):
    per = chunk[1]
    rows = 8 * per
    matrix = pl.BlockSpec((1, NR, NR), lambda c: (c, 0, 0))
    return pl.pallas_call(
        functools.partial(solve_kernel, per, sources, targets),
        grid=(3,),
        in_specs=[whole()] * 8 + [matrix, matrix],
        out_specs=[whole()] * 8,
        out_shape=[piece(per)] * 8,
        scratch_shapes=[pltpu.VMEM((2 * rows, NR), jnp.bfloat16), pltpu.VMEM((rows, NR), jnp.float32)],
        cost_estimate=pl.CostEstimate(flops=3 * 3 * 2 * rows * NR * NR, bytes_accessed=3 * NR * NR * 4 + 2 * 3 * rows * NR * 4, transcendentals=0),
        compiler_params=pltpu.CompilerParams(vmem_limit_bytes=24 * MIB),
        name="solve",
    )(*pieces, hi, lo)


def place_kernel(chunk, group, *refs):
    per = chunk[1]
    pieces, out, sems = refs[: len(group)], refs[-2], refs[-1]
    copies = []
    for n, d in enumerate(group):
        row = pl.multiple_of(row_of(chunk, owner_of(d)), 8)
        for c in range(3):
            copies.append(pltpu.make_async_copy(pieces[n].at[c], out.at[c, :, pl.ds(row, per)], sems.at[n, c]))
    for copy in copies:
        copy.start()
    for copy in copies:
        copy.wait()


def place(chunk, group, pieces, out):
    extra = () if out is None else (out,)
    return pl.pallas_call(
        functools.partial(place_kernel, chunk, group),
        in_specs=[whole()] * len(group) + [in_hbm()] * len(extra),
        out_specs=in_hbm(),
        out_shape=piece(LENGTH),
        scratch_shapes=[pltpu.SemaphoreType.DMA((len(group), 3))],
        input_output_aliases={len(group): 0} if extra else {},
        cost_estimate=pl.CostEstimate(flops=0, bytes_accessed=2 * 3 * 8 * len(group) * chunk[1] * 128 * 4, transcendentals=0),
        compiler_params=pltpu.CompilerParams(vmem_limit_bytes=4 * MIB),
        name="place",
    )(*pieces, *extra)


def exchange(pieces, order):
    return [p if d == 0 else lax.ppermute(p, "rad", [(i, i ^ d) for i in range(8)]) for p, d in zip(pieces, order)]


def per_device(velocity, radial_inverse):
    size = lax.axis_size("theta")
    up = [(i, (i + 1) % size) for i in range(size)]
    below = lax.ppermute(velocity[:, :, LENGTH - 8 :], "theta", up)
    above = lax.ppermute(velocity[:, :, :8], "theta", [(b, a) for a, b in up])
    lane = lax.axis_index("rad") * 128 + jnp.arange(128)
    radius = 1.0 + (lane.astype(jnp.float32) + 0.5) / NR
    c_out = (viscous / 12.0) / radius
    coef = jnp.stack([radius - 30.0 * c_out, c_out] + [radius] * 6)
    count = len(CHUNKS)
    weighted = []
    for chunk, order in zip(CHUNKS, ORDERS):
        pieces = []
        for stop in SPLIT if chunk is CHUNKS[0] else (8,):
            group = order[len(pieces) : stop]
            pieces += stencil(chunk, group, velocity, below, above, coef)
        weighted.append(pieces)
    radial_inverse, weighted[-1][-1] = lax.optimization_barrier((radial_inverse, weighted[-1][-1]))
    arrived = [exchange(pieces, order) for pieces, order in zip(weighted, ORDERS)]
    hi, lo = prepare(radial_inverse)
    out = None
    back = []
    for chunk, pieces, order, target in zip(CHUNKS, arrived, ORDERS, ORDERS[count:]):
        back.append(exchange(solve(chunk, order, target, pieces, hi, lo), target))
    for chunk, pieces, order in zip(CHUNKS, back, ORDERS[count:]):
        start = 0
        for stop in LAST if chunk is CHUNKS[-1] else (8,):
            out = place(chunk, order[start:stop], pieces[start:stop], out)
            start = stop
    return out


def solution(mesh):
    return jax.shard_map(
        per_device,
        mesh=mesh,
        in_specs=(P(None, None, "theta", "rad"), P()),
        out_specs=P(None, None, "theta", "rad"),
        check_vma=False,
    )
```
